32 devices in a mesh: row: 4 (over y, core), col: 8 (over z, x).
Axes of the slice: x: 2, y: 2, z: 4, core: 2. Of those that a mesh axis runs over, the one named last changes fastest.
Arguments:
- pair: bfloat16 [1024, 1024, 128], P('row', 'col'), may hold values from -6 to 6
- norm_gain: float32 [128], replicated, may hold values from 0.1 to 1.9
- norm_shift: float32 [128], replicated, may hold values from -3 to 3
- w_query: bfloat16 [128, 128], replicated, may hold values from -1 to 1
- w_key: bfloat16 [128, 128], replicated, may hold values from -0.5 to 0.5
- w_value: bfloat16 [128, 128], replicated, may hold values from -0.5 to 0.5
- w_gate: bfloat16 [128, 128], replicated, may hold values from -0.5 to 0.5
- gate_shift: float32 [128], replicated, may hold values from -1 to 1
- w_bias: float32 [128, 4], replicated, may hold values from -30 to 30
- w_out: bfloat16 [128, 128], replicated, may hold values from -1 to 1
- out_shift: float32 [128], replicated, may hold values from -3 to 3
Outputs:
- update: bfloat16 [1024, 1024, 128], P('row', 'col')
The draws below stay inside these ranges and needn't reach their ends.
All inputs are finite; a program needn't handle non-finite values.
Results may differ from the reference program's by a relative error of at most 0.0015.
The reference program's roundings to bfloat16 on the way (of `normed`, `query`, `weights` and `gated`) count: a program that leaves them out, or rounds other values in their place, can miss the bound.
Values may be sent and summed in bfloat16 or wider, within the bound.
A program may use at most 128 MiB of HBM per device.

```python
import math
import jax
import jax.numpy as jnp
from jax import lax

N = 1024
C = 128
H = 4
DH = 32


def draw_w_bias(key, part):
    first, second = jax.random.split(jax.random.fold_in(key, 17))
    base = jax.random.truncated_normal(first, -3.0, 3.0, (C, H), jnp.float32) / math.sqrt(C)
    scales = jnp.exp(jax.random.uniform(second, (H,), jnp.float32, math.log(0.5), math.log(2.0)))
    return base * scales[None, :]


def level_of(stream_key, dims, pieces, least, top_value):
    factor_of = 1.0
    for axis_at, shards_of in pieces:
        heights = jax.random.uniform(jax.random.fold_in(jax.random.fold_in(stream_key, 6), axis_at), (shards_of,), jnp.float32, least / len(pieces), top_value / len(pieces))
        factor_of = factor_of * jnp.repeat(jnp.exp(heights), dims[axis_at] // shards_of).reshape((-1,) + (1,) * (len(dims) - 1 - axis_at))
    return factor_of


def gaussian(key, shape, scale, most, pieces=(), dtype=jnp.bfloat16):
    entries = scale * jax.random.normal(key, shape, jnp.float32)
    if pieces:
        entries = entries * level_of(key, shape, pieces, -0.22, 0.18)
    return jnp.clip(entries, -most, most).astype(dtype)


def setup_inputs(seed: int = 0) -> dict:
    key_of = jax.random.split(jax.random.key(seed), 12)
    return {
        "pair": gaussian(key_of[0], (N, N, C), 1.0, 6.0, ((0, 4), (1, 8))),
        "norm_gain": jnp.clip(1.0 + 0.18 * jax.random.normal(key_of[1], (C,), jnp.float32), 0.1, 1.9),
        "norm_shift": gaussian(key_of[2], (C,), 0.3, 3.0, (), jnp.float32),
        "w_query": gaussian(key_of[3], (C, H * DH), 0.18, 1.0),
        "w_key": gaussian(key_of[4], (C, H * DH), C ** -0.5, 0.5),
        "w_value": gaussian(key_of[5], (C, H * DH), C ** -0.5, 0.5),
        "w_gate": gaussian(key_of[6], (C, H * DH), C ** -0.5, 0.5),
        "gate_shift": jnp.clip(jax.random.uniform(key_of[7], (H * DH,), jnp.float32, -1.0, 1.0), -1.0, 1.0),
        "w_bias": draw_w_bias(jax.random.fold_in(key_of[11], 71), 0),
        "w_out": gaussian(key_of[9], (H * DH, C), (H * DH // 4) ** -0.5, 1.0),
        "out_shift": gaussian(key_of[10], (C,), 0.5, 3.0, (), jnp.float32),
    }


def normalize(values, gain, shift):
    values = values.astype(jnp.float32)
    mean = lax.optimization_barrier(jnp.mean(values, axis=-1, keepdims=True))
    centred = values - mean
    spread = lax.optimization_barrier(jnp.mean(centred * centred, axis=-1, keepdims=True))
    return (centred * lax.rsqrt(spread + 1e-05) * gain + shift).astype(jnp.bfloat16)

def reference(pair, norm_gain, norm_shift, w_query, w_key, w_value, w_gate, gate_shift, w_bias, w_out, out_shift):
    normed = normalize(pair, norm_gain, norm_shift)
    bias = jnp.einsum('jkc,ch->hjk', normed.astype(jnp.float32), w_bias, precision=lax.Precision.HIGHEST)
    heads = w_bias.shape[1]
    inner = w_query.shape[1]
    depth = inner // heads
    seq_length = normed.shape[1]

    def one_row(pair_row):
        query = (jnp.dot(pair_row, w_query, preferred_element_type=jnp.float32) * (1.0 / math.sqrt(depth))).astype(jnp.bfloat16)
        key = jnp.dot(pair_row, w_key, preferred_element_type=jnp.float32).astype(jnp.bfloat16)
        value = jnp.dot(pair_row, w_value, preferred_element_type=jnp.float32).astype(jnp.bfloat16)
        gate = jax.nn.sigmoid(jnp.dot(pair_row, w_gate, preferred_element_type=jnp.float32) + gate_shift)
        query = query.reshape(seq_length, heads, depth).astype(jnp.float32)
        key = key.reshape(seq_length, heads, depth).astype(jnp.float32)
        value = value.reshape(seq_length, heads, depth).astype(jnp.float32)
        scores = jnp.einsum('jhd,khd->hjk', query, key) + bias
        largest = lax.optimization_barrier(jnp.max(scores, axis=2, keepdims=True))
        raised = jnp.exp(scores - largest)
        weights = (raised / lax.optimization_barrier(jnp.sum(raised, axis=2, keepdims=True))).astype(jnp.bfloat16)
        attended = jnp.einsum('hjk,khd->jhd', weights.astype(jnp.float32), value).reshape(seq_length, inner)
        gated = (gate * attended).astype(jnp.bfloat16)
        return (jnp.dot(gated, w_out, preferred_element_type=jnp.float32) + out_shift).astype(jnp.bfloat16)
    return lax.map(one_row, normed)
```

```python
import functools
import math

import jax
import jax.numpy as jnp
from jax import lax
from jax.experimental import pallas as pl
from jax.experimental.pallas import tpu as pltpu
from jax.sharding import PartitionSpec as P

F32 = jnp.float32
BF16 = jnp.bfloat16
VMEM_LIMIT = 62 * 1024 * 1024


def nt_dot(a, b):
    return lax.dot_general(a, b, (((1,), (1,)), ((), ())), preferred_element_type=F32)


def norm_body(pair_ref, gain_ref, shift_ref, wbt_ref, normed_ref, bias_ref):
    rows, cols, channels = pair_ref.shape
    heads = bias_ref.shape[0]
    values = pair_ref[...].reshape(rows * cols, channels).astype(F32)
    mean = jnp.mean(values, axis=-1, keepdims=True)
    centred = values - mean
    spread = jnp.mean(centred * centred, axis=-1, keepdims=True)
    normed = (centred * lax.rsqrt(spread + 1e-05) * gain_ref[...] + shift_ref[...]).astype(BF16)
    normed_ref[...] = normed.reshape(rows, cols, channels)
    wbt = wbt_ref[...]
    high = wbt.astype(BF16)
    rest = wbt - high.astype(F32)
    mid = rest.astype(BF16)
    low = (rest - mid.astype(F32)).astype(BF16)
    bias = nt_dot(high, normed) + (nt_dot(mid, normed) + nt_dot(low, normed))
    for j in range(rows):
        bias_ref[:, j, :] = bias[:heads, j * cols : (j + 1) * cols]


def normalize(pair, gain, shift, w_bias):
    tile_rows, tile_cols, channels = pair.shape
    heads = w_bias.shape[1]
    pad = -heads % 16
    wbt = jnp.pad(w_bias.T, ((0, pad), (0, 0)))
    step = 16
    return pl.pallas_call(
        norm_body,
        grid=(tile_rows // step,),
        in_specs=[
            pl.BlockSpec((step, tile_cols, channels), lambda i: (i, 0, 0)),
            pl.BlockSpec((1, channels), lambda i: (0, 0)),
            pl.BlockSpec((1, channels), lambda i: (0, 0)),
            pl.BlockSpec(wbt.shape, lambda i: (0, 0)),
        ],
        out_specs=[
            pl.BlockSpec((step, tile_cols, channels), lambda i: (i, 0, 0)),
            pl.BlockSpec((heads, step, tile_cols), lambda i: (0, i, 0)),
        ],
        out_shape=[
            jax.ShapeDtypeStruct(pair.shape, BF16),
            jax.ShapeDtypeStruct((heads, tile_rows, tile_cols), F32),
        ],
        name="norm_bias",
    )(pair, gain[None], shift[None], wbt)


def project(x, wq_ref, wkt_ref, wv_ref, q_ref, kt_ref, v_ref, heads):
    inner = wq_ref.shape[1]
    depth = inner // heads
    query = (jnp.dot(x, wq_ref[...], preferred_element_type=F32) * (1.0 / math.sqrt(depth)))
    value = jnp.dot(x, wv_ref[...], preferred_element_type=F32)
    kt_ref[...] = nt_dot(wkt_ref[...], x).astype(BF16)
    head_of = lax.broadcasted_iota(jnp.int32, query.shape, 1) // depth
    for h in range(heads):
        q_ref[h] = jnp.where(head_of == h, query, 0.0).astype(BF16)
        v_ref[h] = jnp.where(head_of == h, value, 0.0).astype(BF16)


def attend_block(x, start, size, bias_of, q_ref, kt_ref, v_ref, wg, gshift, wo, oshift, heads):
    attended = None
    for h in range(heads):
        scores = jnp.dot(
            q_ref[h, pl.ds(start, size), :], kt_ref[...], preferred_element_type=F32
        ) + bias_of(h)
        largest = jnp.max(scores, axis=1, keepdims=True)
        raised = jnp.exp(scores - largest)
        scale = 1.0 / jnp.sum(raised, axis=1, keepdims=True)
        weights = (raised * scale).astype(BF16)
        part = jnp.dot(weights, v_ref[h], preferred_element_type=F32)
        attended = part if attended is None else attended + part
    gate = jax.nn.sigmoid(jnp.dot(x, wg, preferred_element_type=F32) + gshift)
    gated = (gate * attended).astype(BF16)
    return (jnp.dot(gated, wo, preferred_element_type=F32) + oshift).astype(BF16)


def attend_body(
    x_ref, bias_ref, wq_ref, wkt_ref, wv_ref, wg_ref, gshift_ref, wo_ref, oshift_ref,
    out_ref, q_ref, kt_ref, v_ref, x_flat, o_flat, *, block,
):
    pieces, heads = bias_ref.shape[0], bias_ref.shape[1]
    length, channels = x_flat.shape
    x_flat[...] = x_ref[...].reshape(length, channels)
    project(x_flat[...], wq_ref, wkt_ref, wv_ref, q_ref, kt_ref, v_ref, heads)

    @pl.loop(0, length // block)
    def _(b):
        start = pl.multiple_of(b * block, block)

        def bias_of(h):
            parts = [bias_ref[p, h, pl.ds(start, block), :] for p in range(pieces)]
            return parts[0] if pieces == 1 else jnp.concatenate(parts, axis=1)

        o_flat[pl.ds(start, block), :] = attend_block(
            x_flat[pl.ds(start, block), :], start, block, bias_of, q_ref, kt_ref, v_ref,
            wg_ref[...], gshift_ref[...], wo_ref[...], oshift_ref[...], heads,
        )

    out_ref[...] = o_flat[...].reshape(out_ref.shape)


def attend(rows, bias, w_query, w_key, w_value, w_gate, gate_shift, w_out, out_shift, block=512):
    groups, count, cols, channels = rows.shape
    length = groups * cols
    heads = bias.shape[1]
    inner = w_query.shape[1]
    whole = lambda a: pl.BlockSpec(a.shape, lambda i: (0,) * a.ndim, pipeline_mode=pl.Buffered(1))
    args = (bias, w_query, w_key.T, w_value, w_gate, gate_shift[None], w_out, out_shift[None])
    row_spec = pl.BlockSpec((groups, 1, cols, channels), lambda i: (0, i, 0, 0))
    return pl.pallas_call(
        functools.partial(attend_body, block=block),
        grid=(count,),
        in_specs=[row_spec] + [whole(a) for a in args],
        out_specs=row_spec,
        out_shape=jax.ShapeDtypeStruct(rows.shape, BF16),
        scratch_shapes=[
            pltpu.VMEM((heads, length, inner), BF16),
            pltpu.VMEM((inner, length), BF16),
            pltpu.VMEM((heads, length, inner), BF16),
            pltpu.VMEM((length, channels), BF16),
            pltpu.VMEM((length, channels), BF16),
        ],
        compiler_params=pltpu.CompilerParams(vmem_limit_bytes=VMEM_LIMIT),
        name="attend",
    )(rows, *args)


def on_device(
    pair, norm_gain, norm_shift, w_query, w_key, w_value, w_gate, gate_shift, w_bias, w_out,
    out_shift,
):
    col_count = lax.axis_size("col")
    row_count = lax.axis_size("row")
    tile_rows, tile_cols, channels = pair.shape
    heads = w_bias.shape[1]
    normed, tile_bias = normalize(pair, norm_gain, norm_shift, w_bias)
    by_row = lax.all_gather(tile_bias, "row", axis=1, tiled=True)
    bias = lax.all_gather(by_row, "col", axis=0)
    if tile_cols % 128:
        bias = bias.transpose(1, 2, 0, 3).reshape(1, heads, tile_rows * row_count, -1)
    blocks = normed.reshape(col_count, tile_rows // col_count, tile_cols, channels)
    rows = lax.all_to_all(blocks, "col", split_axis=0, concat_axis=0, tiled=True)
    update = attend(rows, bias, w_query, w_key, w_value, w_gate, gate_shift, w_out, out_shift)
    back = lax.all_to_all(update, "col", split_axis=0, concat_axis=0, tiled=True)
    return back.reshape(tile_rows, tile_cols, channels)


def solution(mesh):
    in_specs = (P("row", "col", None),) + (P(),) * 10
    return jax.shard_map(
        on_device, mesh=mesh, in_specs=in_specs, out_specs=P("row", "col", None), check_vma=False
    )
```
